32 devices in a mesh: cfg: 2 (over y), space: 16 (over z, x, core).
Axes of the slice: x: 2, y: 2, z: 4, core: 2. Of those that a mesh axis runs over, the one named last changes fastest.
Arguments:
- vectors: bfloat16 [2, 3, 128, 16384], P(None, None, None, ('cfg', 'space')), parts along dimension 3, may hold values from -12 to 12
- links: bfloat16 [3, 2, 3, 3, 16384], P(None, None, None, None, ('cfg', 'space')), parts along dimension 4, may hold values from -2.5 to 2.5
- momenta: int32 [8, 3], replicated, may hold values from -2 to 2, as said below
- displacements: int32 [8], replicated, may hold values from 0 to 2
- perambulators: bfloat16 [4, 2, 128, 32768], P(None, None, None, ('cfg', 'space')), parts along dimension 3, may hold values from -0.059814453 to 0.059814453
Outputs:
- smeared: bfloat16 [2, 3, 128, 16384], P(None, None, None, ('cfg', 'space')), parts along dimension 3
- correlator: float32 [4, 8, 256], P(None, None, ('cfg', 'space')), parts along dimension 2
The draws below stay inside these ranges and needn't reach their ends.
There are 2 independent parts, one for each index of `cfg`. The reference program is written for one: setup_inputs(seed, part) draws one part's arguments, and reference() takes and returns one part's arrays. A program takes and returns all parts, laid end to end along the dimension named above; an argument that names none is the same for every part. Nothing has to cross between parts.
Inputs may be any that keep to these rules, and one draw needn't show every extreme that they name: `momenta`: the first component of every momentum is nonzero.
All inputs are finite; a program needn't handle non-finite values.
Results may differ from the reference program's by a relative error of at most 0.0091.
Values may be sent and summed in bfloat16 or wider, within the bound.
No kernel may reach another device: no remote copies, remote signals or barrier semaphores. Data moves between devices by JAX's collectives and lax.ppermute only.
A program may use at most 128 MiB of HBM per device.

```python
import math
import jax
import jax.numpy as jnp
from jax import lax

TG = 8
LX = 16
LY = 16
ZB = 2
VECTOR_COUNT = 128
MOM = 8
HOPS = 4
SPINP = 16
SPB = 8
SITES = 8192
N_SPACE = 16


def draw_momenta(key, part):
    first_key, second_key, third_key = jax.random.split(jax.random.fold_in(key, 17), 3)
    magnitude = jax.random.randint(first_key, (MOM, 1), 1, 3)
    direction = 2 * jax.random.randint(second_key, (MOM, 1), 0, 2) - 1
    others = jax.random.randint(third_key, (MOM, 2), -2, 3)
    return jnp.concatenate([magnitude * direction, others], axis=1).astype(jnp.int32)


def plant(entries, own_key, smallest, top_value):
    longest = entries.shape.index(max(entries.shape))
    spots = []
    for shift in (0, 1):
        where = [jax.random.randint(jax.random.fold_in(own_key, axis), (), 0, length) for axis, length in enumerate(entries.shape)]
        where[longest] = (where[longest] + shift) % entries.shape[longest]
        spots.append(tuple(where))
    return entries.at[spots[0]].set(smallest).at[spots[1]].set(top_value)


def steps_of(own_key, dims, pieces, least, top_value):
    loudness, own = 1.0, jax.random.fold_in(own_key, 6)
    for axis_at, parts in pieces:
        steps = jnp.exp(jax.random.uniform(jax.random.fold_in(own, axis_at), (parts,), jnp.float32, least / len(pieces), top_value / len(pieces)))
        loudness = loudness * jnp.repeat(steps, dims[axis_at] // parts).reshape([-1 if axis == axis_at else 1 for axis in range(len(dims))])
    return loudness


def centred(stream_key, shape, width, most, shards=(), held_as=jnp.bfloat16):
    loudness = steps_of(stream_key, shape, shards, -0.22, 0.18) if shards else 1.0
    array = jax.random.normal(stream_key, shape, jnp.float32) * width * loudness
    return jnp.minimum(jnp.maximum(array, -most), most).astype(held_as)


def setup_inputs(seed: int = 0, part: int = 0) -> dict:
    key_list = jax.random.split(jax.random.key(seed), 6)
    own_keys = jax.random.split(jax.random.fold_in(key_list[5], part), 6)
    return {
        "vectors": centred(own_keys[0], (2, 3, VECTOR_COUNT, SITES), 2.0, 12.0, ((3, 16),)),
        "links": centred(own_keys[1], (3, 2, 3, 3, SITES), 0.41, 2.5, ((4, 16),)),
        "momenta": draw_momenta(jax.random.fold_in(key_list[5], 71), part),
        "displacements": plant(jax.random.randint(key_list[3], (MOM,), 0, 3), jax.random.fold_in(key_list[3], 1), 0, 2).astype(jnp.int32),
        "perambulators": centred(own_keys[4], (HOPS, 2, VECTOR_COUNT, N_SPACE * SPB * VECTOR_COUNT), 0.01, 0.059814453, ((3, 16),)),
    }


KAPPA = 0.1

def round_trip(values):
    return lax.optimization_barrier(values.astype(jnp.bfloat16)).astype(jnp.float32)

def link_apply(link_re, link_im, vec_re, vec_im, adjoint):
    outs_re = []
    outs_im = []
    for colour_out in range(3):
        total_re = None
        total_im = None
        for colour_in in range(3):
            if adjoint:
                mat_re = link_re[colour_in, colour_out]
                mat_im = -link_im[colour_in, colour_out]
            else:
                mat_re = link_re[colour_out, colour_in]
                mat_im = link_im[colour_out, colour_in]
            term_re = mat_re[None] * vec_re[colour_in] - mat_im[None] * vec_im[colour_in]
            term_im = mat_re[None] * vec_im[colour_in] + mat_im[None] * vec_re[colour_in]
            if total_re is None:
                total_re, total_im = (term_re, term_im)
            else:
                total_re = total_re + term_re
                total_im = total_im + term_im
        outs_re.append(total_re)
        outs_im.append(total_im)
    return (jnp.stack(outs_re), jnp.stack(outs_im))

def phase_angle(momentum, coord_x, coord_y, coord_z, extent_z):
    frac = (momentum[0] * coord_x % LX).astype(jnp.float32) / LX
    frac = frac + (momentum[1] * coord_y % LY).astype(jnp.float32) / LY
    frac = frac + (momentum[2] * coord_z % extent_z).astype(jnp.float32) / extent_z
    return 2.0 * math.pi * frac

def smear(field, lattice):
    total_re = (1.0 - 6.0 * KAPPA) * field[0]
    total_im = (1.0 - 6.0 * KAPPA) * field[1]
    for axis_code in range(3):
        spatial = 4 - axis_code
        link = lattice[axis_code]
        ahead_re, ahead_im = link_apply(link[0], link[1], jnp.roll(field[0], -1, spatial), jnp.roll(field[1], -1, spatial), False)
        behind = jnp.roll(link, 1, spatial + 1)
        back_re, back_im = link_apply(behind[0], behind[1], jnp.roll(field[0], 1, spatial), jnp.roll(field[1], 1, spatial), True)
        total_re = total_re + KAPPA * (ahead_re + back_re)
        total_im = total_im + KAPPA * (ahead_im + back_im)
    return jnp.stack([total_re, total_im])

def reference(vectors, links, momenta, displacements, perambulators):
    blocks = N_SPACE // TG
    extent_z = ZB * blocks
    spins = SPINP // blocks
    scale = 1.0 / math.sqrt(LX * LY * extent_z)
    vec_t = vectors.reshape(2, 3, VECTOR_COUNT, blocks, TG, ZB, LY, LX)
    vec_t = jnp.transpose(vec_t, (4, 0, 1, 2, 3, 5, 6, 7)).reshape(TG, 2, 3, VECTOR_COUNT, extent_z, LY, LX)
    link_t = links.reshape(3, 2, 3, 3, blocks, TG, ZB, LY, LX)
    link_t = jnp.transpose(link_t, (5, 0, 1, 2, 3, 4, 6, 7, 8)).reshape(TG, 3, 2, 3, 3, extent_z, LY, LX)
    coord_x = lax.broadcasted_iota(jnp.int32, (extent_z, LY, LX), 2)
    coord_y = lax.broadcasted_iota(jnp.int32, (extent_z, LY, LX), 1)
    coord_z = lax.broadcasted_iota(jnp.int32, (extent_z, LY, LX), 0)

    def one_slice(operand):
        vec_slice, link_slice = operand
        lattice = link_slice.astype(jnp.float32)
        first = round_trip(smear(vec_slice.astype(jnp.float32), lattice))
        smeared_bf = lax.optimization_barrier(smear(first, lattice).astype(jnp.bfloat16))
        wide = smeared_bf.astype(jnp.float32)
        moved = []
        for axis_code in range(3):
            spatial = 4 - axis_code
            link = lattice[axis_code]
            moved_re, moved_im = link_apply(link[0], link[1], jnp.roll(wide[0], -1, spatial), jnp.roll(wide[1], -1, spatial), False)
            moved.append(round_trip(jnp.stack([moved_re, moved_im])))
        displaced = jnp.stack(moved)

        def operator(pair):
            momentum, direction = pair
            angle = phase_angle(momentum, coord_x, coord_y, coord_z, extent_z)
            cosine = jnp.cos(angle)
            sine = jnp.sin(angle)
            chosen = lax.dynamic_index_in_dim(displaced, direction, 0, keepdims=False)
            phased_re = round_trip(cosine * chosen[0] + sine * chosen[1])
            phased_im = round_trip(cosine * chosen[1] - sine * chosen[0])
            part_re = jnp.einsum('ckzyx,clzyx->kl', wide[0], phased_re) + jnp.einsum('ckzyx,clzyx->kl', wide[1], phased_im)
            part_im = jnp.einsum('ckzyx,clzyx->kl', wide[0], phased_im) - jnp.einsum('ckzyx,clzyx->kl', wide[1], phased_re)
            return jnp.concatenate([part_re, part_im], axis=1) * scale
        elemental = lax.map(operator, (momenta, displacements))
        return (smeared_bf, elemental)
    smeared_t, elementals = lax.map(one_slice, (vec_t, link_t))
    smeared = smeared_t.reshape(TG, 2, 3, VECTOR_COUNT, blocks, ZB, LY, LX)
    smeared = jnp.transpose(smeared, (1, 2, 3, 4, 0, 5, 6, 7)).reshape(2, 3, VECTOR_COUNT, N_SPACE * ZB * LY * LX)
    elem = round_trip(elementals)
    tau = perambulators.reshape(HOPS, 2, VECTOR_COUNT, blocks, TG, spins, VECTOR_COUNT)
    tau = jnp.transpose(tau, (0, 4, 3, 5, 1, 2, 6)).reshape(HOPS, TG, SPINP, 2, VECTOR_COUNT, VECTOR_COUNT).astype(jnp.float32)
    sink_re = elem[..., :VECTOR_COUNT]
    sink_im = elem[..., VECTOR_COUNT:]
    results = []
    for neighbour_index in range(HOPS):
        perambulator_real = tau[neighbour_index, :, :, 0]
        perambulator_imaginary = tau[neighbour_index, :, :, 1]
        product_real = jnp.einsum('tmak,tskl->tmsal', sink_re, perambulator_real) - jnp.einsum('tmak,tskl->tmsal', sink_im, perambulator_imaginary)
        product_imaginary = jnp.einsum('tmak,tskl->tmsal', sink_re, perambulator_imaginary) + jnp.einsum('tmak,tskl->tmsal', sink_im, perambulator_real)
        product_real = round_trip(product_real)
        product_imaginary = round_trip(product_imaginary)
        sandwich_real = jnp.einsum('ehwy,ebhwd->ebhyd', perambulator_real, product_real) + jnp.einsum('ehwy,ebhwd->ebhyd', perambulator_imaginary, product_imaginary)
        sandwich_imaginary = jnp.einsum('ehwy,ebhwd->ebhyd', perambulator_real, product_imaginary) - jnp.einsum('ehwy,ebhwd->ebhyd', perambulator_imaginary, product_real)
        source_vector = jnp.roll(elem, neighbour_index + 1, axis=0)
        entry_value = lax.optimization_barrier(jnp.sum(sandwich_real * source_vector[:, :, None, :, :VECTOR_COUNT], axis=(3, 4))) + lax.optimization_barrier(jnp.sum(sandwich_imaginary * source_vector[:, :, None, :, VECTOR_COUNT:], axis=(3, 4)))
        entry_value = jnp.transpose(entry_value.reshape(TG, MOM, blocks, spins), (1, 2, 0, 3)).reshape(MOM, N_SPACE * spins)
        results.append(entry_value)
    return (smeared, jnp.stack(results))
```

```python
import functools
import math

import jax
import jax.numpy as jnp
import numpy as np
from jax import lax
from jax.experimental import pallas as pl
from jax.experimental.pallas import tpu as pltpu
from jax.sharding import PartitionSpec as P

TG = 8
LX = 16
LY = 16
HOPS = 4


KAPPA = 0.1


def passed_along(shard, axis, by):
    peers = lax.axis_size(axis)
    return lax.ppermute(shard, axis, [(i, (i + by) % peers) for i in range(peers)])


def partner_2(shard, axis, apart):
    return lax.ppermute(shard, axis, [(i, i ^ 1 << apart) for i in range(lax.axis_size(axis))])


def link_apply(link_re, link_im, vec_re, vec_im, adjoint):
    outs_re = []
    outs_im = []
    for colour_out in range(3):
        total_re = None
        total_im = None
        for colour_in in range(3):
            if adjoint:
                mat_re = link_re[colour_in, colour_out]
                mat_im = -link_im[colour_in, colour_out]
            else:
                mat_re = link_re[colour_out, colour_in]
                mat_im = link_im[colour_out, colour_in]
            term_re = mat_re[None] * vec_re[colour_in] - mat_im[None] * vec_im[colour_in]
            term_im = mat_re[None] * vec_im[colour_in] + mat_im[None] * vec_re[colour_in]
            if total_re is None:
                total_re, total_im = (term_re, term_im)
            else:
                total_re = total_re + term_re
                total_im = total_im + term_im
        outs_re.append(total_re)
        outs_im.append(total_im)
    return (jnp.stack(outs_re), jnp.stack(outs_im))


def phase_angle(momentum, coord_x, coord_y, coord_z, extent_z):
    frac = (momentum[0] * coord_x % LX).astype(jnp.float32) / LX
    frac = frac + (momentum[1] * coord_y % LY).astype(jnp.float32) / LY
    frac = frac + (momentum[2] * coord_z % extent_z).astype(jnp.float32) / extent_z
    return 2.0 * math.pi * frac


def beside(field, axis_code, offset):
    last = field.ndim - 1
    if axis_code == 1:
        return jnp.roll(field, -offset * LX, last)
    column = lax.broadcasted_iota(jnp.int32, (field.shape[-1],), 0) % LX
    if offset > 0:
        return jnp.where(column == LX - 1, jnp.roll(field, LX - 1, last), jnp.roll(field, -1, last))
    return jnp.where(column == 0, jnp.roll(field, 1 - LX, last), jnp.roll(field, 1, last))


def smear_block(v_ext, links_here, z_below):
    centre = v_ext[:, :, :, 1:-1]
    total_re = (1.0 - 6.0 * KAPPA) * centre[0]
    total_im = (1.0 - 6.0 * KAPPA) * centre[1]
    for axis_code in range(2):
        link = links_here[axis_code]
        ahead_re, ahead_im = link_apply(
            link[0],
            link[1],
            beside(centre[0], axis_code, 1),
            beside(centre[1], axis_code, 1),
            False,
        )
        behind = beside(link, axis_code, -1)
        back_re, back_im = link_apply(
            behind[0],
            behind[1],
            beside(centre[0], axis_code, -1),
            beside(centre[1], axis_code, -1),
            True,
        )
        total_re = total_re + KAPPA * (ahead_re + back_re)
        total_im = total_im + KAPPA * (ahead_im + back_im)
    link = links_here[2]
    ahead_re, ahead_im = link_apply(link[0], link[1], v_ext[0, :, :, 2:], v_ext[1, :, :, 2:], False)
    behind = jnp.concatenate([z_below, link[:, :, :, :-1]], axis=3)
    back_re, back_im = link_apply(
        behind[0], behind[1], v_ext[0, :, :, :-2], v_ext[1, :, :, :-2], True
    )
    total_re = total_re + KAPPA * (ahead_re + back_re)
    total_im = total_im + KAPPA * (ahead_im + back_im)
    return jnp.stack([total_re, total_im])


def from_below(payload):
    return passed_along(payload, "space", TG)


def from_above(payload):
    return passed_along(payload, "space", -TG)


def partner(values, bit_place):
    return partner_2(values, "space", bit_place)


def body_many(vectors, links, momenta, displacements, perambulators):
    vector_count = vectors.shape[2]
    plane = LX * LY
    depth = vectors.shape[3] // plane
    blocks = lax.axis_size("space") // TG
    block = lax.axis_index("space") // TG
    field = vectors.reshape(2, 3, vector_count, depth, plane)
    lattice = links.reshape(3, 2, 3, 3, depth, plane)
    wide_links = lattice.astype(jnp.float32)
    rows_vec = 6 * vector_count
    current = field
    for sweep in range(2):
        lower = from_below(
            jnp.concatenate(
                [
                    current[:, :, :, -1:].reshape(-1, plane),
                    lattice[2, :, :, :, -1:].reshape(-1, plane),
                ],
                axis=0,
            )
        )
        upper = from_above(current[:, :, :, :1].reshape(-1, plane))
        v_ext = jnp.concatenate(
            [
                lower[:rows_vec].reshape(2, 3, vector_count, 1, plane),
                current,
                upper.reshape(2, 3, vector_count, 1, plane),
            ],
            axis=3,
        ).astype(jnp.float32)
        z_below = lower[rows_vec:].reshape(2, 3, 3, 1, plane).astype(jnp.float32)
        current = smear_block(v_ext, wide_links, z_below).astype(jnp.bfloat16)
    smeared = current
    upper = from_above(smeared[:, :, :, :1].reshape(-1, plane)).reshape(
        2, 3, vector_count, 1, plane
    )
    wide = smeared.astype(jnp.float32)
    raised = jnp.concatenate([smeared, upper], axis=3)[:, :, :, 1:].astype(jnp.float32)
    moved = []
    for axis_code in range(3):
        link = wide_links[axis_code]
        if axis_code < 2:
            ahead_re = beside(wide[0], axis_code, 1)
            ahead_im = beside(wide[1], axis_code, 1)
        else:
            ahead_re = raised[0]
            ahead_im = raised[1]
        moved_re, moved_im = link_apply(link[0], link[1], ahead_re, ahead_im, False)
        moved.append(jnp.stack([moved_re, moved_im]).astype(jnp.bfloat16))
    displaced = jnp.stack(moved)
    position = lax.broadcasted_iota(jnp.int32, (depth, plane), 1)
    coord_x = position % LX
    coord_y = position // LX
    coord_z = lax.broadcasted_iota(jnp.int32, (depth, plane), 0) + block * depth
    extent_z = depth * blocks
    scale = 1.0 / math.sqrt(LX * LY * extent_z)
    contract = (((0, 1, 3, 4), (0, 1, 3, 4)), ((), ()))

    def operator(pair):
        momentum, direction = pair
        angle = phase_angle(momentum, coord_x, coord_y, coord_z, extent_z)
        cosine = jnp.cos(angle)
        sine = jnp.sin(angle)
        chosen = lax.dynamic_index_in_dim(displaced, direction, 0, keepdims=False).astype(
            jnp.float32
        )
        phased_re = (cosine * chosen[0] + sine * chosen[1]).astype(jnp.bfloat16)
        phased_im = (cosine * chosen[1] - sine * chosen[0]).astype(jnp.bfloat16)
        real_part = lax.dot_general(
            smeared, jnp.stack([phased_re, phased_im]), contract, preferred_element_type=jnp.float32
        )
        imag_part = lax.dot_general(
            smeared,
            jnp.stack([phased_im, -phased_re]),
            contract,
            preferred_element_type=jnp.float32,
        )
        return jnp.concatenate([real_part, imag_part], axis=1) * scale

    partial_sum = lax.map(operator, (momenta, displacements))
    levels = blocks.bit_length() - 1
    base = TG.bit_length() - 1
    piece = partial_sum
    for level in range(levels):
        upper_bit = block >> level & 1
        half = piece.shape[1] // 2
        lower_half = piece[:, :half]
        upper_half = piece[:, half:]
        keep = jnp.where(upper_bit == 1, upper_half, lower_half)
        sending = jnp.where(upper_bit == 1, lower_half, upper_half)
        piece = keep + partner(sending, base + level)
    for level in reversed(range(levels)):
        upper_bit = block >> level & 1
        other = partner(piece, base + level)
        piece = jnp.where(
            upper_bit == 1,
            jnp.concatenate([other, piece], axis=1),
            jnp.concatenate([piece, other], axis=1),
        )
    elem = piece.astype(jnp.bfloat16)
    operators = elem.shape[0]
    spins = perambulators.shape[3] // vector_count
    left = elem.reshape(-1, 2 * vector_count)
    sandwich_list = []
    for neighbour_index in range(HOPS):
        perambulator_real = perambulators[neighbour_index, 0]
        perambulator_imaginary = perambulators[neighbour_index, 1]
        right = jnp.concatenate(
            [
                jnp.concatenate([perambulator_real, perambulator_imaginary], axis=1),
                jnp.concatenate([-perambulator_imaginary, perambulator_real], axis=1),
            ],
            axis=0,
        )
        product = jnp.dot(left, right, preferred_element_type=jnp.float32).astype(jnp.bfloat16)
        product = product.reshape(operators, vector_count, 2, spins, vector_count)
        tau_re3 = perambulator_real.reshape(vector_count, spins, vector_count)
        tau_im3 = perambulator_imaginary.reshape(vector_count, spins, vector_count)
        sandwich_real = jnp.einsum(
            "asp,masl->mspl", tau_re3, product[:, :, 0], preferred_element_type=jnp.float32
        )
        sandwich_real = sandwich_real + jnp.einsum(
            "asp,masl->mspl", tau_im3, product[:, :, 1], preferred_element_type=jnp.float32
        )
        sandwich_imaginary = jnp.einsum(
            "asp,masl->mspl", tau_re3, product[:, :, 1], preferred_element_type=jnp.float32
        )
        sandwich_imaginary = sandwich_imaginary - jnp.einsum(
            "asp,masl->mspl", tau_im3, product[:, :, 0], preferred_element_type=jnp.float32
        )
        sandwich_list.append((sandwich_real, sandwich_imaginary))
    arrived = elem
    results = []
    for neighbour_index in range(HOPS):
        arrived = passed_along(arrived, "space", 1)
        source_vector = arrived.astype(jnp.float32)
        sandwich_real, sandwich_imaginary = sandwich_list[neighbour_index]
        entry_value = jnp.sum(
            sandwich_real * source_vector[:, None, :, :vector_count], axis=(2, 3)
        ) + jnp.sum(sandwich_imaginary * source_vector[:, None, :, vector_count:], axis=(2, 3))
        results.append(entry_value)
    return (smeared.reshape(2, 3, vector_count, depth * plane), jnp.stack(results))


COMPONENTS = 6
SLOTS = 40
WIDE = SLOTS * LX
USED = 32 * LX
MIB = 1 << 20
VMEM = pl.BlockSpec(memory_space=pltpu.VMEM)
SMEM = pl.BlockSpec(memory_space=pltpu.SMEM)


def hop_slots():
    slots = {}
    for q in range(COMPONENTS):
        slots[q] = ("xf", q)
        slots[8 + q] = ("zf", q)
        slots[16 + q] = ("yf", q)
        slots[24 + q] = ("zb", q)
        slots[32 + q] = ("xb", q)
        slots[(6, 7, 14, 15, 22, 23)[q]] = ("yb", q)
    return slots


def stencil_constants():
    pick = np.zeros((COMPONENTS, 80, WIDE), np.float32)
    where = np.zeros((8, WIDE), np.int32)
    near = np.zeros((LX, WIDE), np.float32)
    for slot, (hop, q_in) in hop_slots().items():
        lanes = slice(slot * LX, (slot + 1) * LX)
        part_in, colour_in = divmod(q_in, 3)
        axis = "xyz".index(hop[0])
        columns = np.arange(LX)
        where[0, lanes] = (columns - 1) % LX if hop == "xf" else columns
        where[1, lanes] = 1 if hop == "yb" else 0
        shift = {"xf": 1, "xb": -1}.get(hop, 0)
        for x_out in range(LX):
            near[x_out, slot * LX + (x_out + shift) % LX] = 1.0
        for q_out in range(COMPONENTS):
            part_out, colour_out = divmod(q_out, 3)
            mixed = int(part_in != part_out)
            if hop[1] == "f":
                a, b = colour_out, colour_in
                sign = -1.0 if (part_out, part_in) == (0, 1) else 1.0
            else:
                a, b = colour_in, colour_out
                sign = -1.0 if (part_out, part_in) == (1, 0) else 1.0
            row = ((axis * 2 + mixed) * 3 + a) * 3 + b
            if hop == "zb":
                row = 54 + (mixed * 3 + a) * 3 + b
            pick[q_out, row, lanes] = sign
    return pick, where, near


def stencil_kernel(links_ref, pick_ref, where_ref, near_ref, full_ref, ahead_ref):
    planes = links_ref.shape[0]
    plane = links_ref.shape[2]
    ones = jnp.ones((LX, 80), jnp.bfloat16)

    def one_row(y, carry):
        row = y - where_ref[1:2, :]
        row = jnp.where(row < 0, row + LY, row)
        source = row * LX + where_ref[0:1, :]
        spread = (
            lax.broadcasted_iota(jnp.int32, (plane, WIDE), 0) == jnp.broadcast_to(source, (plane, WIDE))
        )
        spread = jnp.where(spread, 1.0, 0.0).astype(jnp.bfloat16)
        for z in range(planes):
            laid = jnp.dot(links_ref[z], spread, preferred_element_type=jnp.float32).astype(jnp.bfloat16)
            for q in range(COMPONENTS):
                line = jnp.dot(ones, laid * pick_ref[q], preferred_element_type=jnp.float32)
                line = line * near_ref[...]
                rows = slice(q * LX, (q + 1) * LX)
                first = line[:, : 8 * LX]
                ahead_ref[z * LY + y, rows, :] = first.astype(jnp.bfloat16)
                full_ref[z * LY + y, rows, : 8 * LX] = (first + line[:, USED:]).astype(jnp.bfloat16)
                full_ref[z * LY + y, rows, 8 * LX :] = line[:, 8 * LX : USED].astype(jnp.bfloat16)
        return carry

    lax.fori_loop(0, LY, one_row, 0)


def smear_kernel(
    own_ref, other_ref, full_ref, ahead_ref, smeared_ref, wide_ref, moved_ref, start, first, last
):
    rows = full_ref.shape[0]
    planes = rows // LY
    half = own_ref.shape[1]
    sites = rows * LX
    vector_count = own_ref.shape[3]
    start[:, :half] = own_ref[...]
    start[:, half:] = other_ref[...]
    zero = jnp.zeros((LX, vector_count), jnp.bfloat16)
    slots = hop_slots()

    def places(z, y):
        up = jnp.where(y == LY - 1, 0, y + 1)
        down = jnp.where(y == 0, LY - 1, y - 1)
        above = (z + 1) % planes
        below = (z - 1) % planes
        return {
            "xf": z * LY + y,
            "yf": z * LY + up,
            "yb": z * LY + down,
            "zf": above * LY + y,
            "zb": below * LY + y,
        }

    def gathered(ref, place, wanted, hops):
        pieces = []
        for slot in wanted:
            hop, q = slots.get(slot, (None, 0))
            pieces.append(ref[q, place[hop]] if hop in hops else zero)
        return jnp.concatenate(pieces, axis=0)

    def sweep(source, target):
        def one_row(y, carry):
            for z in range(planes):
                place = places(z, y)
                r = z * LY + y
                around = gathered(source, place, range(32), ("xf", "yf", "yb", "zf", "zb"))
                total = jnp.dot(full_ref[r], around, preferred_element_type=jnp.float32)
                for q in range(COMPONENTS):
                    value = (1.0 - 6.0 * KAPPA) * source[q, r].astype(jnp.float32)
                    value = value + KAPPA * total[q * LX : (q + 1) * LX]
                    target[q, r] = value.astype(jnp.bfloat16)
            return carry

        lax.fori_loop(0, LY, one_row, 0)

    sweep(start, first)
    sweep(first, last)

    def displace(y, carry):
        for z in range(planes):
            place = places(z, y)
            r = z * LY + y
            for axis, (hop, begin) in enumerate((("xf", 0), ("yf", 16), ("zf", 8))):
                around = gathered(last, place, range(begin, begin + 8), (hop,))
                if axis == 0:
                    matrix = ahead_ref[r]
                else:
                    matrix = full_ref[r, :, begin * LX : (begin + 8) * LX]
                total = jnp.dot(matrix, around, preferred_element_type=jnp.float32)
                for q in range(COMPONENTS):
                    moved_ref[axis, q, r] = total[q * LX : (q + 1) * LX].astype(jnp.bfloat16)
        return carry

    lax.fori_loop(0, LY, displace, 0)
    for q in range(COMPONENTS):
        for b in range(sites // 128):
            tile = last[q, b * 8 : (b + 1) * 8].reshape(128, vector_count)
            tile = jnp.transpose(tile)
            wide_ref[:, q * sites + b * 128 : q * sites + (b + 1) * 128] = tile
            if b * 8 < half:
                smeared_ref[q, :, b * 128 : (b + 1) * 128] = tile


def elemental_kernel(
    offset, scale, direction_ref, row_cos_ref, row_sin_ref, cos_ref, sin_ref, wide_ref, moved_ref, out_ref, phased
):
    rows = moved_ref.shape[2]
    sites = rows * LX
    vector_count = moved_ref.shape[4]
    for index in range(out_ref.shape[0]):
        m = offset + index
        direction = direction_ref[m]
        base_cos = cos_ref[m]
        base_sin = sin_ref[m]

        def one_row(r, carry):
            turn_cos = row_cos_ref[m, r]
            turn_sin = row_sin_ref[m, r]
            cosine = base_cos * turn_cos - base_sin * turn_sin
            sine = base_sin * turn_cos + base_cos * turn_sin
            for c in range(3):
                real = moved_ref[direction, c, r].astype(jnp.float32)
                imag = moved_ref[direction, 3 + c, r].astype(jnp.float32)
                phased_re = cosine * real + sine * imag
                phased_im = cosine * imag - sine * real
                upper = pl.ds(pl.multiple_of(c * sites + r * LX, LX), LX)
                lower = pl.ds(pl.multiple_of((3 + c) * sites + r * LX, LX), LX)
                phased[index % 2, upper, :vector_count] = phased_re.astype(jnp.bfloat16)
                phased[index % 2, upper, vector_count:] = phased_im.astype(jnp.bfloat16)
                phased[index % 2, lower, :vector_count] = phased_im.astype(jnp.bfloat16)
                phased[index % 2, lower, vector_count:] = (-phased_re).astype(jnp.bfloat16)
            return carry

        lax.fori_loop(0, rows, one_row, 0, unroll=4)
        total = jnp.dot(wide_ref[...], phased[index % 2], preferred_element_type=jnp.float32)
        out_ref[index] = (total * scale).astype(jnp.bfloat16)


def right_kernel(elem_ref, tau_ref, out_ref):
    operators, vector_count, wide = elem_ref.shape
    left = elem_ref[...].reshape(operators * vector_count, wide)
    spins = tau_ref.shape[3] // vector_count
    for s in range(spins):
        lanes = slice(s * vector_count, (s + 1) * vector_count)
        real = tau_ref[0, 0, :, lanes]
        imag = tau_ref[0, 1, :, lanes]
        right = jnp.concatenate(
            [jnp.concatenate([real, imag], axis=1), jnp.concatenate([-imag, real], axis=1)], axis=0
        )
        out_ref[0, s] = jnp.dot(left, right, preferred_element_type=jnp.float32).astype(jnp.bfloat16)


def trace_kernel(which_ref, source_ref, tau_ref, product_ref, out_ref):
    operators, vector_count, wide = source_ref.shape[1:]
    spins = tau_ref.shape[3] // vector_count
    left = jnp.concatenate(
        [
            jnp.concatenate(
                [
                    tau_ref[0, part, :, s * vector_count : (s + 1) * vector_count]
                    for part in range(2)
                ],
                axis=1,
            )
            for s in range(spins)
        ],
        axis=0,
    )

    def one_operator(m, carry):
        top = source_ref[0, m]
        bottom = jnp.concatenate([-top[:, vector_count:], top[:, :vector_count]], axis=1)
        right = jnp.concatenate([top, bottom], axis=0)
        other = jnp.dot(left, right, preferred_element_type=jnp.float32)
        lines = []
        for s in range(spins):
            rows = pl.ds(pl.multiple_of(m * vector_count, vector_count), vector_count)
            mine = product_ref[0, s, rows, :].astype(jnp.float32)
            both = mine * other[s * vector_count : (s + 1) * vector_count]
            both = jnp.sum(both.reshape(vector_count // 8, 8, wide), axis=0)
            both = both[:, :vector_count] + both[:, vector_count:]
            lines.append(jnp.sum(both, axis=0, keepdims=True))
        out_ref[0, m] = jnp.concatenate(lines, axis=0)
        return carry

    lax.fori_loop(0, operators, one_operator, 0)


def swapped(values, bit):
    return partner_2(values, "space", bit)


def correlators(elem, perambulators):
    operators, vector_count, wide = elem.shape
    spins = perambulators.shape[3] // vector_count
    index = lax.axis_index("space")
    core = index & 1
    column = index >> 1 & 1
    back_4 = swapped(elem, 2)
    back_2 = swapped(jnp.where(column == 0, elem, back_4), 1)
    early = swapped(jnp.where(core == 0, elem, back_4), 0)
    late = swapped(back_2, 0)
    tau_spec = pl.BlockSpec((1, 2, vector_count, spins * vector_count), lambda h: (h, 0, 0, 0))
    products = pl.pallas_call(
        right_kernel,
        grid=(HOPS,),
        in_specs=[pl.BlockSpec((operators, vector_count, wide), lambda h: (0, 0, 0)), tau_spec],
        out_specs=pl.BlockSpec((1, spins, operators * vector_count, wide), lambda h: (h, 0, 0, 0)),
        out_shape=jax.ShapeDtypeStruct((HOPS, spins, operators * vector_count, wide), jnp.bfloat16),
        compiler_params=pltpu.CompilerParams(vmem_limit_bytes=40 * MIB),
        cost_estimate=pl.CostEstimate(flops=4_300_000_000, bytes_accessed=20_000_000, transcendentals=0),
        name="right",
    )(elem, perambulators)

    def traces(sources, hops):
        count = len(sources)
        which = jnp.stack([jnp.int32(h) for h in hops])
        stacked = jnp.stack(sources)
        return pl.pallas_call(
            trace_kernel,
            grid_spec=pltpu.PrefetchScalarGridSpec(
                num_scalar_prefetch=1,
                grid=(count,),
                in_specs=[
                    pl.BlockSpec((1, operators, vector_count, wide), lambda g, w: (g, 0, 0, 0)),
                    pl.BlockSpec((1, 2, vector_count, spins * vector_count), lambda g, w: (w[g], 0, 0, 0)),
                    pl.BlockSpec((1, spins, operators * vector_count, wide), lambda g, w: (w[g], 0, 0, 0)),
                ],
                out_specs=pl.BlockSpec((1, operators, spins, vector_count), lambda g, w: (g, 0, 0, 0)),
            ),
            out_shape=jax.ShapeDtypeStruct((count, operators, spins, vector_count), jnp.float32),
            compiler_params=pltpu.CompilerParams(vmem_limit_bytes=40 * MIB),
            cost_estimate=pl.CostEstimate(
                flops=1_070_000_000 * count, bytes_accessed=5_000_000 * count, transcendentals=0
            ),
            name="traces",
        )(which, stacked, perambulators, products)

    part_a = traces([back_4, early], [3, jnp.where(core == 0, 2, 0)])
    part_b = traces([back_2, late], [1, jnp.where(core == 0, 0, 2)])
    lines = jnp.stack(
        [
            jnp.where(core == 0, part_b[1], part_a[1]),
            part_b[0],
            jnp.where(core == 0, part_a[1], part_b[1]),
            part_a[0],
        ]
    )
    return jnp.sum(lines, axis=-1)


def body_pair(vectors, links, momenta, displacements, perambulators):
    vector_count = vectors.shape[2]
    plane = LX * LY
    depth = vectors.shape[3] // plane
    blocks = lax.axis_size("space") // TG
    block = lax.axis_index("space") // TG
    planes = depth * blocks
    rows = planes * LY
    half = depth * LY
    sites = planes * plane
    operators = momenta.shape[0]
    other_links = from_below(links)
    own = jnp.transpose(vectors.reshape(COMPONENTS, vector_count, depth * plane), (0, 2, 1))
    own = own.reshape(COMPONENTS, half, LX, vector_count)
    other = from_below(own)

    lattice = jnp.concatenate(
        [links.reshape(54, depth, plane), other_links.reshape(54, depth, plane)], axis=1
    )
    lattice = jnp.transpose(lattice, (1, 0, 2))
    lattice = jnp.concatenate(
        [
            lattice,
            jnp.roll(lattice[:, 36:], 1, 0),
            jnp.zeros((planes, 8, plane), jnp.bfloat16),
        ],
        axis=1,
    )
    pick, where, near = stencil_constants()
    full, ahead = pl.pallas_call(
        stencil_kernel,
        in_specs=[VMEM] * 4,
        out_specs=[VMEM] * 2,
        out_shape=[
            jax.ShapeDtypeStruct((rows, COMPONENTS * LX, USED), jnp.bfloat16),
            jax.ShapeDtypeStruct((rows, COMPONENTS * LX, 8 * LX), jnp.bfloat16),
        ],
        compiler_params=pltpu.CompilerParams(vmem_limit_bytes=24 * MIB),
        cost_estimate=pl.CostEstimate(flops=15_000_000_000, bytes_accessed=9_000_000, transcendentals=0),
        name="stencil",
    )(lattice, jnp.asarray(pick, jnp.bfloat16), where, near)

    smeared, wide, moved = pl.pallas_call(
        smear_kernel,
        in_specs=[VMEM] * 4,
        out_specs=[VMEM] * 3,
        out_shape=[
            jax.ShapeDtypeStruct((COMPONENTS, vector_count, depth * plane), jnp.bfloat16),
            jax.ShapeDtypeStruct((vector_count, COMPONENTS * sites), jnp.bfloat16),
            jax.ShapeDtypeStruct((3, COMPONENTS, rows, LX, vector_count), jnp.bfloat16),
        ],
        scratch_shapes=[pltpu.VMEM((COMPONENTS, rows, LX, vector_count), jnp.bfloat16)] * 3,
        compiler_params=pltpu.CompilerParams(vmem_limit_bytes=36 * MIB),
        cost_estimate=pl.CostEstimate(flops=5_000_000_000, bytes_accessed=16_000_000, transcendentals=0),
        name="smear",
    )(own, other, full, ahead)

    x_frac = (momenta[:, 0:1] * lax.iota(jnp.int32, LX)[None] % LX).astype(jnp.float32) / LX
    x_angle = jnp.broadcast_to((2.0 * math.pi * x_frac)[:, :, None], (operators, LX, vector_count))
    row = lax.iota(jnp.int32, rows)[None]
    coord_y = row % LY
    coord_z = (row // LY + block * depth) % planes
    row_angle = (momenta[:, 1:2] * coord_y % LY).astype(jnp.float32) / LY
    row_angle = row_angle + (momenta[:, 2:3] * coord_z % planes).astype(jnp.float32) / planes
    row_angle = 2.0 * math.pi * row_angle
    scale = 1.0 / math.sqrt(sites)
    pieces = []
    chunk = operators
    for offset in range(0, operators, chunk):
        pieces.append(
            pl.pallas_call(
                functools.partial(elemental_kernel, offset, scale),
                in_specs=[SMEM] * 3 + [VMEM] * 4,
                out_specs=VMEM,
                out_shape=jax.ShapeDtypeStruct((chunk, vector_count, 2 * vector_count), jnp.bfloat16),
                scratch_shapes=[pltpu.VMEM((2, COMPONENTS * sites, 2 * vector_count), jnp.bfloat16)],
                compiler_params=pltpu.CompilerParams(vmem_limit_bytes=30 * MIB),
                cost_estimate=pl.CostEstimate(
                    flops=400_000_000 * chunk, bytes_accessed=7_000_000, transcendentals=0
                ),
                name="elementals",
            )(
                displacements,
                jnp.cos(row_angle),
                jnp.sin(row_angle),
                jnp.cos(x_angle),
                jnp.sin(x_angle),
                wide,
                moved,
            )
        )
    elem = pieces[0]
    return (
        smeared.reshape(2, 3, vector_count, depth * plane),
        correlators(elem, perambulators),
    )


def solution(mesh):
    placed = (
        P(None, None, None, ("cfg", "space")),
        P(None, None, None, None, ("cfg", "space")),
        P(),
        P(),
        P(None, None, None, ("cfg", "space")),
    )
    blocks = mesh.shape["space"] // TG
    return jax.shard_map(
        body_pair if blocks == 2 else body_many,
        mesh=mesh,
        in_specs=placed,
        out_specs=(P(None, None, None, ("cfg", "space")), P(None, None, ("cfg", "space"))),
        check_vma=False,
    )
```
